32 devices in a mesh: pipe: 4 (over y, core), tensor: 8 (over z, x).
Axes of the slice: x: 2, y: 2, z: 4, core: 2. Of those that a mesh axis runs over, the one named last changes fastest.
Arguments:
- saved_inputs: bfloat16 [4, 4, 64, 4096], P('pipe', None, 'tensor'), may hold values from -6 to 6
- gate_weight: bfloat16 [4, 4096, 12288], P('pipe', None, 'tensor'), may hold values from -0.09375 to 0.09375
- up_weight: bfloat16 [4, 4096, 12288], P('pipe', None, 'tensor'), may hold values from -0.09375 to 0.09375
- down_weight: bfloat16 [4, 12288, 4096], P('pipe', 'tensor'), may hold values from -0.0546875 to 0.0546875
- section_grads: bfloat16 [4, 64, 4096], P('pipe', 'tensor'), may hold values from -6 to 6
- loss_grad: bfloat16 [64, 4096], P('tensor'), may hold values from -6 to 6
- trainable: int32 [1], replicated, may hold values from 0 to 255
- slot_table: int32 [2, 4], replicated, may hold values from 0 to 3, as said below
Outputs:
- input_grads: bfloat16 [2, 4, 64, 4096], P(None, 'pipe', 'tensor')
- grad_gate: bfloat16 [4096, 12288], P('pipe', 'tensor')
- grad_up: bfloat16 [4096, 12288], P('pipe', 'tensor')
- grad_down: bfloat16 [12288, 4096], P('tensor', 'pipe')
The draws below stay inside these ranges and needn't reach their ends.
Inputs may be any that keep to these rules, and one draw needn't show every extreme that they name: `slot_table`: in each tick every one of the 4 slots is picked by some section.
All inputs are finite; a program needn't handle non-finite values.
Results may differ from the reference program's by a relative error of at most 0.006.
Values may be sent and summed in bfloat16 or wider, within the bound.
No kernel may reach another device: no remote copies, remote signals or barrier semaphores. Data moves between devices by JAX's collectives and lax.ppermute only.
A program may use at most 128 MiB of HBM per device.

```python
import jax
import jax.numpy as jnp
from jax import lax

D = 4096
FF = 12288
SLOTS = 4
TOK = 64
SECTIONS = 4


def draw_slot_table(key, part):
    base = jnp.arange(SECTIONS, dtype=jnp.int32) % SLOTS
    first = jax.random.permutation(jax.random.fold_in(key, 11), base)
    second = jax.random.permutation(jax.random.fold_in(key, 23), base)
    return jnp.stack([first, second]).astype(jnp.int32)


def levels(own_key, extent, pieces, low, top_value):
    factor_of, own = 1.0, jax.random.fold_in(own_key, 6)
    for position, blocks in pieces:
        draws = jnp.exp(jax.random.uniform(jax.random.fold_in(own, position), (blocks,), jnp.float32, low / len(pieces), top_value / len(pieces)))
        factor_of = factor_of * jnp.repeat(draws, extent[position] // blocks).reshape([-1 if axis == position else 1 for axis in range(len(extent))])
    return factor_of


def normal_values(stream_key, shape, spread, bound, cuts=(), kind=jnp.bfloat16):
    values = spread * jax.random.normal(stream_key, shape, jnp.float32)
    if cuts:
        values = values * levels(stream_key, shape, cuts, -0.22, 0.18)
    return jnp.clip(values, -bound, bound).astype(kind)


def setup_inputs(seed: int = 0) -> dict:
    streams_of = jax.random.split(jax.random.key(seed), 9)
    return {
        "saved_inputs": normal_values(streams_of[0], (SECTIONS, SLOTS, TOK, D), 1.0, 6.0, ((0, 4), (2, 8))),
        "gate_weight": normal_values(streams_of[1], (SECTIONS, D, FF), D ** -0.5, 0.09375, ((0, 4), (2, 8))),
        "up_weight": normal_values(streams_of[2], (SECTIONS, D, FF), D ** -0.5, 0.09375, ((0, 4), (2, 8))),
        "down_weight": normal_values(streams_of[3], (SECTIONS, FF, D), FF ** -0.5, 0.0546875, ((0, 4), (1, 8))),
        "section_grads": normal_values(streams_of[4], (SECTIONS, TOK, D), 1.0, 6.0, ((0, 4), (1, 8))),
        "loss_grad": normal_values(streams_of[5], (TOK, D), 1.0, 6.0, ((0, 8),)),
        "trainable": jax.random.randint(streams_of[6], (1,), 0, 64 * SECTIONS).astype(jnp.int32),
        "slot_table": draw_slot_table(jax.random.fold_in(streams_of[8], 71), 0),
    }


def contract_rows(left, right):
    return lax.dot_general(left, right, (((0,), (0,)), ((), ())), preferred_element_type=jnp.float32)


def contract_cols(left, right):
    return lax.dot_general(left, right, (((1,), (1,)), ((), ())), preferred_element_type=jnp.float32)


def backward_local(inputs_full, out_full, w_gate, w_up, w_down):
    gate_pre = jnp.dot(inputs_full, w_gate, preferred_element_type=jnp.float32)
    up_pre = jnp.dot(inputs_full, w_up, preferred_element_type=jnp.float32)
    sigmoid_gate = jax.nn.sigmoid(gate_pre)
    silu_gate = gate_pre * sigmoid_gate
    hidden = (silu_gate * up_pre).astype(jnp.bfloat16)
    hidden_grad = contract_cols(out_full, w_down)
    gate_grad = (hidden_grad * up_pre * sigmoid_gate * (1.0 + gate_pre * (1.0 - sigmoid_gate))).astype(jnp.bfloat16)
    up_grad = (hidden_grad * silu_gate).astype(jnp.bfloat16)
    return hidden, gate_grad, up_grad


def section_backward(operands):
    inputs_full, out_full, w_gate, w_up, w_down = operands
    hidden, gate_grad, up_grad = backward_local(inputs_full, out_full, w_gate, w_up, w_down)
    in_grad = (contract_cols(gate_grad, w_gate) + contract_cols(up_grad, w_up)).astype(jnp.bfloat16)
    return in_grad, hidden, gate_grad, up_grad


def reference(saved_inputs, gate_weight, up_weight, down_weight, section_grads, loss_grad, trainable, slot_table):
    section_ids = jnp.arange(SECTIONS)
    inputs_one = saved_inputs[section_ids, slot_table[0]]
    first = lax.map(section_backward, (inputs_one, section_grads, gate_weight, up_weight, down_weight))
    out_two = jnp.concatenate([first[0][1:], loss_grad[None]], axis=0)
    inputs_two = saved_inputs[section_ids, slot_table[1]]
    second = lax.map(section_backward, (inputs_two, out_two, gate_weight, up_weight, down_weight))
    input_grads = jnp.stack([first[0], second[0]])
    owner = (trainable[0] % SECTIONS).astype(jnp.int32)

    def pick(stack_one, stack_two):
        return jnp.concatenate([lax.dynamic_index_in_dim(stack_one, owner, 0, keepdims=False),
                                lax.dynamic_index_in_dim(stack_two, owner, 0, keepdims=False)], axis=0)

    inputs_all = pick(inputs_one, inputs_two)
    out_all = pick(section_grads, out_two)
    hidden_all = pick(first[1], second[1])
    gate_all = pick(first[2], second[2])
    up_all = pick(first[3], second[3])
    grad_gate = contract_rows(inputs_all, gate_all).astype(jnp.bfloat16)
    grad_up = contract_rows(inputs_all, up_all).astype(jnp.bfloat16)
    grad_down = contract_rows(hidden_all, out_all).astype(jnp.bfloat16)
    return input_grads, grad_gate, grad_up, grad_down
```

```python
import functools

import jax
import jax.numpy as jnp
from jax import lax
from jax.experimental import pallas as pl
from jax.experimental.pallas import tpu as pltpu
from jax.sharding import PartitionSpec as P


BF16 = jnp.bfloat16
F32 = jnp.float32
VM = pl.BlockSpec(memory_space=pltpu.VMEM)
SM = pl.BlockSpec(memory_space=pltpu.SMEM)
MIB = 1 << 20
INNER = 4


def dot_rows(a, b):
    return lax.dot_general(a, b, (((0,), (0,)), ((), ())), preferred_element_type=F32)


def dot_mid(a, b):
    return lax.dot_general(a, b, (((1,), (0,)), ((), ())), preferred_element_type=F32)


def dot_cols(a, b):
    return lax.dot_general(a, b, (((1,), (1,)), ((), ())), preferred_element_type=F32)


def call(kernel, outs, *args, scratch=(), limit=12, flops=0, smem=1, name=None):
    size = sum(a.size * a.dtype.itemsize for a in args)
    return pl.pallas_call(
        kernel,
        out_shape=tuple(jax.ShapeDtypeStruct(s, d) for s, d in outs),
        in_specs=[SM] * smem + [VM] * (len(args) - smem),
        out_specs=tuple(VM for _ in outs),
        scratch_shapes=list(scratch),
        compiler_params=pltpu.CompilerParams(vmem_limit_bytes=limit * MIB),
        cost_estimate=pl.CostEstimate(flops=flops, bytes_accessed=size, transcendentals=0),
        name=name,
    )(*args)


def xor_pairs(n, k):
    return [(i, i ^ k) for i in range(n) if i ^ k < n]


def chunk_of(size, top):
    return next(c for c in (top, 1024, 768, 512, 384, 256, 128) if c <= top and size % c == 0)


def columns(index, width):
    return pl.ds(pl.multiple_of(index * width, width), width)


class Sizes:
    def __init__(self, saved, w_gate):
        self.n = lax.axis_size("tensor")
        self.p = lax.axis_size("pipe")
        self.inner = min(INNER, self.n)
        self.outer = self.n // self.inner
        self.r = saved.shape[2]
        self.d, self.f = w_gate.shape
        self.tok = self.n * self.r
        self.ticks = 2
        self.cb = self.d // self.inner
        self.pb = self.d // self.p

    def slot(self, k, o):
        return k ^ (o * self.inner)


def spread_rows(part, z):
    got = [part] + [
        lax.ppermute(part, "tensor", xor_pairs(z.n, o * z.inner)) for o in range(1, z.outer)
    ]
    held = jnp.stack(got)
    return [held] + [lax.ppermute(held, "tensor", xor_pairs(z.n, k)) for k in range(1, z.inner)]


def fill(z, pieces, dest, parts):
    for k, piece in enumerate(pieces):
        for o in range(z.outer):
            for part in range(parts):
                at = part * z.tok + z.slot(k, o) * z.r
                dest[at : at + z.r, :] = piece[o, part]


def first_hidden_grad(z, sc, *refs):
    pieces, (w_down, out, dy) = refs[: z.inner], refs[z.inner :]
    fill(z, pieces, dy, 1)
    step = chunk_of(z.f, 768)
    for c in range(0, z.f, step):
        out[:, c : c + step] = dot_cols(dy[...], w_down[c : c + step, :])


def to_sections(z, s, src, rows, at, group_refs):
    for g, ref in enumerate(group_refs):
        low = 0 if g == 0 else 1 << (g - 1)
        for i in range(ref.shape[0]):
            ref[i, at : at + rows, :] = src[:, columns(s ^ (low + i), z.pb)]


def forward(z, sc, *refs):
    pieces = refs[: z.inner]
    dy_pieces = refs[z.inner : 2 * z.inner]
    w_gate, w_up, hg, acts, a_next, b_next, *rest = refs[2 * z.inner :]
    groups, (x, dy) = rest[:-2], rest[-2:]
    fill(z, pieces, x, z.ticks)
    fill(z, dy_pieces, dy, 1)
    rows, tok = z.ticks * z.tok, z.tok
    step = chunk_of(z.f, 512)
    for c in range(0, z.f, step):
        at = slice(c, c + step)
        gate = dot_mid(x[...], w_gate[:, at])
        up = dot_mid(x[...], w_up[:, at])
        sg = jax.nn.sigmoid(gate)
        silu = gate * sg
        slope = up * sg * (1.0 + gate * (1.0 - sg))
        acts[0:rows, at] = (silu * up).astype(BF16)
        acts[rows : rows + tok, at] = (hg[:, at] * slope[:tok]).astype(BF16)
        acts[rows + tok : rows + 2 * tok, at] = (hg[:, at] * silu[:tok]).astype(BF16)
        a_next[:, at] = slope[tok:]
        b_next[:, at] = silu[tok:]
    to_sections(z, sc[1], x, rows, 0, groups)
    to_sections(z, sc[1], dy, tok, rows, groups)


def first_back(z, k, sc, acts, w_gate, w_up, out):
    rows = z.ticks * z.tok
    at = columns(sc[0] ^ k, z.cb)
    y = dot_cols(acts[rows : rows + z.tok, :], w_gate[at, :])
    y += dot_cols(acts[rows + z.tok : rows + 2 * z.tok, :], w_up[at, :])
    for j in range(z.n):
        out[j] = y[j * z.r : (j + 1) * z.r].astype(out.dtype)


def sum_inner(z, sc, own, *refs):
    got, out = refs[:-1], refs[-1]
    for j in range(z.n):
        total = own[j]
        for k in range(1, z.inner):
            total += got[k - 1][j ^ k].astype(F32)
        out[j] = total.astype(BF16)


def sum_outer(z, sc, *refs):
    got, out = refs[:-1], refs[-1]
    for j in range(z.n):
        total = got[0][j].astype(F32)
        for o in range(1, z.outer):
            total += got[o][j ^ (o * z.inner)].astype(F32)
        out[j] = total.astype(BF16)


def second_hidden(z, sc, *refs):
    blocks = refs[: z.inner]
    loss = refs[z.inner : 2 * z.inner]
    w_down, a_next, b_next, acts, back, *rest = refs[2 * z.inner :]
    groups, dy = rest[:-1], rest[-1]
    for k, block in enumerate(blocks):
        at = columns(sc[0] ^ k, z.cb)
        for j in range(z.n):
            dy[j * z.r : (j + 1) * z.r, at] = block[j ^ k]
    back[...] = dy[0 : z.r, :]

    @pl.when(sc[2] == 1)
    def _():
        fill(z, loss, dy, 1)

    step = chunk_of(z.f, 768)
    for c in range(0, z.f, step):
        at = slice(c, c + step)
        hg = dot_cols(dy[...], w_down[at, :])
        acts[0 : z.tok, at] = (hg * a_next[:, at]).astype(BF16)
        acts[z.tok : 2 * z.tok, at] = (hg * b_next[:, at]).astype(BF16)
    to_sections(z, sc[1], dy, z.tok, 0, groups)


def second_back(z, sc, acts, w_gate, w_up, *outs):
    step = chunk_of(z.d, 1024)
    for c in range(0, z.d, step):
        y = dot_cols(acts[0 : z.tok, :], w_gate[c : c + step, :])
        y += dot_cols(acts[z.tok : 2 * z.tok, :], w_up[c : c + step, :])
        for k in range(z.inner):
            for o in range(z.outer):
                at = z.slot(k, o) * z.r
                outs[k][o, :, c : c + step] = y[at : at + z.r].astype(outs[k].dtype)


def sum_rows(z, sc, own, *refs):
    got, (kept, *sent) = refs[: z.inner - 1], refs[z.inner - 1 :]
    for o in range(z.outer):
        total = own[o]
        for piece in got:
            total += piece[o].astype(F32)
        if o == 0:
            kept[...] = total
        else:
            sent[o - 1][...] = total.astype(BF16)


def finish_rows(z, sc, back, kept, *refs):
    got, out = refs[:-1], refs[-1]
    total = kept[...]
    for piece in got:
        total += piece[...].astype(F32)
    out[0, 0] = back[...]
    out[1, 0] = total.astype(BF16)


def choose(z, owner, candidates, dest, at=0):
    for j, ref in enumerate(candidates):

        @pl.when(owner == j)
        def _(ref=ref):
            dest[at : at + ref.shape[0], :] = ref[...]


def weight_grad(z, left_counts, right_counts, sc, *refs):
    p = z.p
    parts = len(left_counts) + len(right_counts)
    refs_in, (out, left, right) = refs[: parts * p], refs[parts * p :]

    @pl.when(pl.program_id(0) == 0)
    def _():
        index, at = 0, 0
        for dest, counts in ((left, left_counts), (right, right_counts)):
            at = 0
            for count in counts:
                choose(z, sc[3], refs_in[index * p : (index + 1) * p], dest, at)
                index += 1
                at += count

    step = out.shape[0]
    at = pl.ds(pl.multiple_of(pl.program_id(0) * step, step), step)
    out[...] = dot_rows(left[:, at], right[...]).astype(BF16)


def call_weight_grad(z, scalars, lefts, rights):
    lc = [part[0].shape[0] for part in lefts]
    rc = [part[0].shape[0] for part in rights]
    rows, cols = lefts[0][0].shape[1], rights[0][0].shape[1]
    step = chunk_of(rows, 256)
    flat = [c for part in lefts + rights for c in part]
    return pl.pallas_call(
        functools.partial(weight_grad, z, lc, rc),
        grid=(rows // step,),
        out_shape=jax.ShapeDtypeStruct((rows, cols), BF16),
        in_specs=[SM] + [VM] * len(flat),
        out_specs=pl.BlockSpec((step, cols), lambda i: (i, 0)),
        scratch_shapes=[pltpu.VMEM((sum(lc), rows), BF16), pltpu.VMEM((sum(rc), cols), BF16)],
        compiler_params=pltpu.CompilerParams(vmem_limit_bytes=12 * MIB),
        cost_estimate=pl.CostEstimate(
            flops=2 * sum(lc) * rows * cols, bytes_accessed=2 * rows * cols, transcendentals=0
        ),
    )(scalars, *flat)


def pipe_bits(z):
    bits = []
    bit = 1
    while bit < z.p:
        bits.append(bit)
        bit *= 2
    return bits[::-1]


def share_all(z, value):
    held = {0: value}
    for bit in pipe_bits(z):
        for j in list(held):
            held[j ^ bit] = lax.ppermute(held[j], "pipe", xor_pairs(z.p, bit))
    return [held[j] for j in range(z.p)]


def share_columns(z, groups):
    held = {0: list(groups)}
    for step, bit in enumerate(pipe_bits(z)):
        for j in list(held):
            *keep, sent = held[j]
            held[j] = keep
            got = lax.ppermute(sent, "pipe", xor_pairs(z.p, bit))
            low = [got[0:1]]
            for g in range(len(keep) - 1):
                low.append(got[1 << g : 2 << g])
            held[j ^ bit] = low
    return [held[j][0][0] for j in range(z.p)]


def group_shapes(z, rows):
    counts = [1] + [b for b in pipe_bits(z)[::-1]]
    return [((c, rows, z.pb), BF16) for c in counts]


def local(saved, gate_weight, up_weight, down_weight, section_grads, loss_grad, trainable, slots):
    w_gate, w_up, w_down = gate_weight[0], up_weight[0], down_weight[0]
    z = Sizes(saved, w_gate)
    s = lax.axis_index("pipe")
    t = lax.axis_index("tensor")
    last = (s == z.p - 1).astype(jnp.int32)
    owner = trainable[0] % z.p
    scalars = jnp.stack([t & (z.inner - 1), s, last, owner ^ s]).astype(jnp.int32)
    run = lambda kernel, *a, **k: call(functools.partial(kernel, z), *a, **k)
    rows = z.ticks * z.tok

    x_rows = jnp.stack(
        [lax.dynamic_index_in_dim(saved[0], slots[k, s], 0, keepdims=False) for k in range(z.ticks)]
    )
    dy_pieces = spread_rows(section_grads, z)
    x_pieces = spread_rows(x_rows, z)

    (hg,) = run(
        first_hidden_grad, [((z.tok, z.f), F32)], scalars, *dy_pieces, w_down,
        scratch=[pltpu.VMEM((z.tok, z.d), BF16)], flops=2 * z.tok * z.d * z.f,
    )
    acts, a_next, b_next, *x_groups = run(
        forward,
        [((rows + 2 * z.tok, z.f), BF16), ((z.tok, z.f), F32), ((z.tok, z.f), F32)]
        + group_shapes(z, rows + z.tok),
        scalars, *x_pieces, *dy_pieces, w_gate, w_up, hg,
        scratch=[pltpu.VMEM((rows, z.d), BF16), pltpu.VMEM((z.tok, z.d), BF16)],
        flops=4 * rows * z.d * z.f,
    )
    got = []
    for k in range(z.inner - 1, -1, -1):
        (part,) = call(
            functools.partial(first_back, z, k),
            [((z.n, z.r, z.cb), BF16 if k else F32)],
            scalars, acts, w_gate, w_up, flops=4 * z.tok * z.d * z.f // z.inner,
        )
        got.append(lax.ppermute(part, "tensor", xor_pairs(z.n, k)) if k else part)
    (half,) = run(sum_inner, [((z.n, z.r, z.cb), BF16)], scalars, got[-1], *got[-2::-1])
    crossed = []
    for o in range(z.outer):
        pairs = [
            (a * z.n + i, (a - 1) % z.p * z.n + (i ^ (o * z.inner)))
            for a in range(z.p)
            for i in range(z.n)
        ]
        crossed.append(lax.ppermute(half, ("pipe", "tensor"), pairs))
    (block,) = run(sum_outer, [((z.n, z.r, z.cb), BF16)], scalars, *crossed)
    blocks = [block] + [
        lax.ppermute(block, "tensor", xor_pairs(z.n, k)) for k in range(1, z.inner)
    ]
    loss_pieces = spread_rows(loss_grad[None], z)
    acts_two, back, *dy_groups = run(
        second_hidden,
        [((2 * z.tok, z.f), BF16), ((z.r, z.d), BF16)] + group_shapes(z, z.tok),
        scalars, *blocks, *loss_pieces, w_down, a_next, b_next,
        scratch=[pltpu.VMEM((z.tok, z.d), BF16)], flops=2 * z.tok * z.d * z.f,
    )
    returned = lax.ppermute(back, "pipe", [(a, (a + 1) % z.p) for a in range(z.p)])
    own, *sent = run(
        second_back,
        [((z.outer, z.r, z.d), BF16 if k else F32) for k in range(z.inner)],
        scalars, acts_two, w_gate, w_up, flops=4 * z.tok * z.d * z.f,
    )
    got = [lax.ppermute(v, "tensor", xor_pairs(z.n, k + 1)) for k, v in enumerate(sent)]
    kept, *sent = run(
        sum_rows, [((z.r, z.d), F32)] + [((z.r, z.d), BF16)] * (z.outer - 1), scalars, own, *got
    )
    got = [
        lax.ppermute(v, "tensor", xor_pairs(z.n, (o + 1) * z.inner)) for o, v in enumerate(sent)
    ]
    (input_grads,) = run(
        finish_rows, [((z.ticks, 1, z.r, z.d), BF16)], scalars, returned, kept, *got
    )

    early = share_all(z, acts)
    x_cols = share_columns(z, x_groups)
    dy_cols = share_columns(z, dy_groups)
    late = share_all(z, acts_two)
    tok = z.tok
    cut = lambda vs, a, b: [v[a:b] for v in vs]
    h_parts = [cut(early, 0, rows)]
    x_parts = [cut(x_cols, 0, rows)]
    dy_parts = [cut(x_cols, rows, rows + tok), dy_cols]
    gg = [cut(early, rows, rows + tok), cut(late, 0, tok)]
    ug = [cut(early, rows + tok, rows + 2 * tok), cut(late, tok, 2 * tok)]
    grad_down = call_weight_grad(z, scalars, h_parts, dy_parts)
    grad_gate = call_weight_grad(z, scalars, x_parts, gg)
    grad_up = call_weight_grad(z, scalars, x_parts, ug)
    return input_grads, grad_gate, grad_up, grad_down


def solution(mesh):
    placed = (
        P("pipe", None, "tensor", None),
        P("pipe", None, "tensor"),
        P("pipe", None, "tensor"),
        P("pipe", "tensor", None),
        P("pipe", "tensor", None),
        P("tensor", None),
        P(),
        P(),
    )
    return jax.shard_map(
        local,
        mesh=mesh,
        in_specs=placed,
        out_specs=(
            P(None, "pipe", "tensor", None),
            P("pipe", "tensor"),
            P("pipe", "tensor"),
            P("tensor", "pipe"),
        ),
        check_vma=False,
    )
```

```python
import functools
import math

import jax
import jax.numpy as jnp
from jax import lax
from jax.experimental import pallas as pl
from jax.experimental.pallas import tpu as pltpu
from jax.sharding import PartitionSpec as P


BF16 = jnp.bfloat16
F32 = jnp.float32
VM = pl.BlockSpec(memory_space=pltpu.VMEM)
SM = pl.BlockSpec(memory_space=pltpu.SMEM)
ANY = pl.BlockSpec(memory_space=pl.ANY)
MIB = 1 << 20
PREFETCH = int(6e9)
INNER = 4


def dot_rows(a, b):
    return lax.dot_general(a, b, (((0,), (0,)), ((), ())), preferred_element_type=F32)


def dot_mid(a, b):
    return lax.dot_general(a, b, (((1,), (0,)), ((), ())), preferred_element_type=F32)


def dot_cols(a, b):
    return lax.dot_general(a, b, (((1,), (1,)), ((), ())), preferred_element_type=F32)


def call(kernel, outs, *args, scratch=(), limit=5242880, flops=0, smem=1, anys=(), name=None):
    size = sum(a.size * a.dtype.itemsize for a in args)
    held = sum(math.prod(v.shape) * 4 for v in scratch if v.shape and len(v.shape) > 1)
    limit += held
    return pl.pallas_call(
        kernel,
        out_shape=tuple(jax.ShapeDtypeStruct(s, d) for s, d in outs),
        in_specs=[
            SM if i < smem else ANY if i in anys else VM for i in range(len(args))
        ],
        out_specs=tuple(VM for _ in outs),
        scratch_shapes=list(scratch),
        compiler_params=pltpu.CompilerParams(vmem_limit_bytes=limit),
        cost_estimate=pl.CostEstimate(flops=flops, bytes_accessed=size, transcendentals=0),
        name=name,
    )(*args)


def xor_pairs(n, k):
    return [(i, i ^ k) for i in range(n) if i ^ k < n]


def chunk_of(size, top):
    return next(c for c in (top, 1024, 768, 512, 384, 256, 128) if c <= top and size % c == 0)


def columns(index, width):
    return pl.ds(pl.multiple_of(index * width, width), width)


class Sizes:
    def __init__(self, saved, w_gate):
        self.n = lax.axis_size("tensor")
        self.p = lax.axis_size("pipe")
        self.inner = min(INNER, self.n)
        self.outer = self.n // self.inner
        self.r = saved.shape[2]
        self.d, self.f = w_gate.shape
        self.tok = self.n * self.r
        self.ticks = 2
        self.cb = self.d // self.inner
        self.pb = self.d // self.p

    def slot(self, k, o):
        return k ^ (o * self.inner)


def pick_rows(z, slots, saved, out, sems):
    s = lax.axis_index("pipe")
    copies = [
        pltpu.make_async_copy(saved.at[slots[k, s]], out.at[k], sems.at[k])
        for k in range(z.ticks)
    ]
    for copy in copies:
        copy.start()
    for copy in copies:
        copy.wait()


def pack(sc, *refs):
    for i, ref in enumerate(refs[:-1]):
        refs[-1][i] = ref[...]


def after(value, earlier):
    return lax.optimization_barrier((value, earlier))[0]


def spread_rows(part, z, scalars, flops=0, sections=None, gate=None):
    sections = range(z.p) if sections is None else sections
    send = lambda v, k: lax.ppermute(
        v,
        ("pipe", "tensor"),
        [(a * z.n + i, a * z.n + j) for a in sections for i, j in xor_pairs(z.n, k)],
    )
    got = [part] + [send(part, o * z.inner) for o in range(1, z.outer)]
    if gate is not None:
        got = [after(v, gate) for v in got]
    (held,) = call(pack, [((z.outer,) + part.shape, BF16)], scalars, *got, flops=flops)
    return [held] + [send(held, k) for k in range(1, z.inner)]


def fill(z, pieces, dest, parts):
    for k, piece in enumerate(pieces):
        for o in range(z.outer):
            for part in range(parts):
                at = part * z.tok + z.slot(k, o) * z.r
                dest[at : at + z.r, :] = piece[o, part]


def fill_apart(z, pieces, dest, parts):
    for k in range(z.inner):
        for o in range(z.outer):
            for part in range(parts):
                at = part * z.tok + z.slot(k, o) * z.r
                dest[at : at + z.r, :] = pieces[k * z.outer + o][part]


def first_hidden_grad(z, sc, *refs):
    pieces, (w_down, out, dy) = refs[: z.inner], refs[z.inner :]
    fill(z, pieces, dy, 1)
    step = chunk_of(z.f, 768)
    for c in range(0, z.f, step):
        out[:, c : c + step] = dot_cols(dy[...], w_down[c : c + step, :])


def to_sections(z, s, src, rows, at, even, odd):
    for j in range(z.p):
        ref = odd if j & 1 else even
        ref[j // 2, at : at + rows, :] = src[:, columns(s ^ j, z.pb)]


def halves(z, s, acts, parts, near, far):
    h = z.tok // 2
    for part in range(parts):
        for ref, which in ((near, s & 1), (far, 1 - (s & 1))):
            at = pl.ds(pl.multiple_of(part * z.tok + which * h, h), h)
            ref[part * h : (part + 1) * h, :] = acts[at, :]


def forward(z, sc, *refs):
    pieces = refs[: z.n]
    dy_pieces = refs[z.n : z.n + z.inner]
    w_gate, w_up, hg, acts, a_next, b_next, near, far, even, odd, x, dy = refs[z.n + z.inner :]
    fill_apart(z, pieces, x, z.ticks)
    fill(z, dy_pieces, dy, 1)
    rows, tok = z.ticks * z.tok, z.tok
    step = chunk_of(z.f, 512)
    for c in range(0, z.f, step):
        at = slice(c, c + step)
        gate = dot_mid(x[...], w_gate[:, at])
        up = dot_mid(x[...], w_up[:, at])
        sg = jax.nn.sigmoid(gate)
        silu = gate * sg
        slope = up * sg * (1.0 + gate * (1.0 - sg))
        acts[0:rows, at] = (silu * up).astype(BF16)
        acts[rows : rows + tok, at] = (hg[:, at] * slope[:tok]).astype(BF16)
        acts[rows + tok : rows + 2 * tok, at] = (hg[:, at] * silu[:tok]).astype(BF16)
        a_next[:, at] = slope[tok:]
        b_next[:, at] = silu[tok:]
    halves(z, sc[1], acts, z.ticks + 2, near, far)
    to_sections(z, sc[1], x, rows, 0, even, odd)
    to_sections(z, sc[1], dy, tok, rows, even, odd)


def first_back(z, k, sc, acts, w_gate, w_up, out):
    rows = z.ticks * z.tok
    at = columns(sc[0] ^ k, z.cb)
    y = dot_cols(acts[rows : rows + z.tok, :], w_gate[at, :])
    y += dot_cols(acts[rows + z.tok : rows + 2 * z.tok, :], w_up[at, :])
    for j in range(z.n):
        out[j] = y[j * z.r : (j + 1) * z.r].astype(out.dtype)


def sum_inner(z, sc, own, *refs):
    got, out = refs[:-1], refs[-1]
    for j in range(z.n):
        total = own[j]
        for k in range(1, z.inner):
            total += got[k - 1][j ^ k].astype(F32)
        out[j] = total.astype(BF16)


def sum_outer(z, sc, *refs):
    got, out = refs[:-1], refs[-1]
    for j in range(z.n):
        total = got[0][j].astype(F32)
        for o in range(1, z.outer):
            total += got[o][j ^ (o * z.inner)].astype(F32)
        out[j] = total.astype(BF16)


def second_hidden(z, sc, *refs):
    blocks = refs[: z.inner]
    loss = refs[z.inner : 2 * z.inner]
    w_down, a_next, b_next, acts, back, near, far, even, odd, dy = refs[2 * z.inner :]
    for k, block in enumerate(blocks):
        at = columns(sc[0] ^ k, z.cb)
        for j in range(z.n):
            dy[j * z.r : (j + 1) * z.r, at] = block[j ^ k]
    back[...] = dy[0 : z.r, :]

    @pl.when(sc[2] == 1)
    def _():
        fill(z, loss, dy, 1)

    step = chunk_of(z.f, 768)
    for c in range(0, z.f, step):
        at = slice(c, c + step)
        hg = dot_cols(dy[...], w_down[at, :])
        acts[0 : z.tok, at] = (hg * a_next[:, at]).astype(BF16)
        acts[z.tok : 2 * z.tok, at] = (hg * b_next[:, at]).astype(BF16)
    halves(z, sc[1], acts, 2, near, far)
    to_sections(z, sc[1], dy, z.tok, 0, even, odd)


def second_back(z, sc, acts, w_gate, w_up, *outs):
    step = chunk_of(z.d, 1024)
    for c in range(0, z.d, step):
        y = dot_cols(acts[0 : z.tok, :], w_gate[c : c + step, :])
        y += dot_cols(acts[z.tok : 2 * z.tok, :], w_up[c : c + step, :])
        for k in range(z.inner):
            for o in range(z.outer):
                at = z.slot(k, o) * z.r
                outs[k][o, :, c : c + step] = y[at : at + z.r].astype(outs[k].dtype)


def sum_rows(z, sc, own, *refs):
    got, (kept, *sent) = refs[: z.inner - 1], refs[z.inner - 1 :]
    for o in range(z.outer):
        total = own[o]
        for piece in got:
            total += piece[o].astype(F32)
        if o == 0:
            kept[...] = total
        else:
            sent[o - 1][...] = total.astype(BF16)


def finish_rows(z, sc, back, kept, *refs):
    got, out = refs[:-1], refs[-1]
    total = kept[...]
    for piece in got:
        total += piece[...].astype(F32)
    out[0, 0] = back[...]
    out[1, 0] = total.astype(BF16)


def select(bit, shift, sc, mine, got, out):
    own = ((sc[3] >> shift) & 1) == 0

    @pl.when(own)
    def _():
        out[...] = mine[...]

    @pl.when(jnp.logical_not(own))
    def _():
        out[...] = got[...]


def call_select(shift, scalars, mine, got):
    (out,) = call(functools.partial(select, 1 << shift, shift), [(mine.shape, BF16)], scalars, mine, got)
    return out


def pipe_shifts(z):
    return range((z.p - 1).bit_length())


def share_halves(z, scalars, near, far, gate=None):
    for shift in pipe_shifts(z):
        got = lax.ppermute(far if shift == 0 else near, "pipe", xor_pairs(z.p, 1 << shift))
        near = call_select(shift, scalars, near, got)
        if shift == 0 and gate is not None:
            near = after(near, gate)
    return near, lax.ppermute(near, "pipe", xor_pairs(z.p, 1))


def share_columns(z, scalars, even, odd, gate=None):
    for shift in pipe_shifts(z):
        got = lax.ppermute(odd, "pipe", xor_pairs(z.p, 1 << shift))
        mine = call_select(shift, scalars, even, got)
        if shift == 0 and gate is not None:
            mine = after(mine, gate)
        even, odd = mine[0::2], mine[1::2]
    return mine[0]


def join(z, s, near, far, part, dest, at):
    h = z.tok // 2
    for ref, which in ((near, s & 1), (far, 1 - (s & 1))):
        dest[pl.ds(pl.multiple_of(at + which * h, h), h), :] = ref[part * h : (part + 1) * h, :]


def down_grad(z, sc, near, far, x_cols, dy_cols, out, left, right):
    rows = z.ticks * z.tok

    @pl.when(pl.program_id(0) == 0)
    def _():
        for k in range(z.ticks):
            join(z, sc[1], near, far, k, left, k * z.tok)
        right[0 : z.tok, :] = x_cols[rows : rows + z.tok, :]
        right[z.tok :, :] = dy_cols[...]

    step = out.shape[0]
    at = pl.ds(pl.multiple_of(pl.program_id(0) * step, step), step)
    out[...] = dot_rows(left[:, at], right[...]).astype(BF16)


def in_grad(z, sc, near, far, near_two, far_two, x_cols, gate_out, up_out, right):
    @pl.when(pl.program_id(0) == 0)
    def _():
        for i in range(2):
            join(z, sc[1], near, far, z.ticks + i, right.at[i], 0)
            join(z, sc[1], near_two, far_two, i, right.at[i], z.tok)

    step = gate_out.shape[0]
    at = pl.ds(pl.multiple_of(pl.program_id(0) * step, step), step)
    left = x_cols[0 : z.ticks * z.tok, at]
    gate_out[...] = dot_rows(left, right[0]).astype(BF16)
    up_out[...] = dot_rows(left, right[1]).astype(BF16)


def call_grad(kernel, shape, count, scratch, scalars, *args):
    rows, cols = shape
    step = chunk_of(rows, 256)
    out = pl.BlockSpec((step, cols), lambda i: (i, 0))
    return pl.pallas_call(
        kernel,
        grid=(rows // step,),
        out_shape=(jax.ShapeDtypeStruct(shape, BF16),) * count,
        in_specs=[SM] + [VM] * len(args),
        out_specs=(out,) * count,
        scratch_shapes=[pltpu.VMEM(v, BF16) for v in scratch],
        compiler_params=pltpu.CompilerParams(vmem_limit_bytes=8 * MIB),
        cost_estimate=pl.CostEstimate(
            flops=256 * count * rows * cols, bytes_accessed=2 * count * rows * cols, transcendentals=0
        ),
    )(scalars, *args)


def local(saved, gate_weight, up_weight, down_weight, section_grads, loss_grad, trainable, slots):
    w_gate, w_up, w_down = gate_weight[0], up_weight[0], down_weight[0]
    z = Sizes(saved, w_gate)
    s = lax.axis_index("pipe")
    t = lax.axis_index("tensor")
    last = (s == z.p - 1).astype(jnp.int32)
    owner = trainable[0] % z.p
    scalars = jnp.stack([t & (z.inner - 1), s, last, owner ^ s]).astype(jnp.int32)
    run = lambda kernel, *a, **k: call(functools.partial(kernel, z), *a, **k)
    rows = z.ticks * z.tok

    (x_rows,) = run(
        pick_rows, [((z.ticks, z.r, z.d), BF16)], slots, saved[0],
        scratch=[pltpu.SemaphoreType.DMA((z.ticks,))], anys=(1,), flops=PREFETCH,
    )
    dy_pieces = spread_rows(section_grads, z, scalars, flops=PREFETCH)
    x_own = [x_rows] + [lax.ppermute(x_rows, "tensor", xor_pairs(z.n, k)) for k in range(1, z.inner)]
    x_all = [[v] for v in x_own]
    for o in range(1, z.outer):
        v = lax.ppermute(x_rows, "tensor", xor_pairs(z.n, o * z.inner))
        x_all[0].append(v)
        for k in range(1, z.inner):
            x_all[k].append(lax.ppermute(v, "tensor", xor_pairs(z.n, k)))
    x_pieces = [v for group in x_all for v in group]

    (hg,) = run(
        first_hidden_grad, [((z.tok, z.f), F32)], scalars, *dy_pieces, w_down,
        scratch=[pltpu.VMEM((z.tok, z.d), BF16)], flops=2 * z.tok * z.d * z.f,
    )
    half_shape = ((rows + 2 * z.tok) // 2, z.f)
    acts, a_next, b_next, near, far, x_even, x_odd = run(
        forward,
        [((rows + 2 * z.tok, z.f), BF16), ((z.tok, z.f), F32), ((z.tok, z.f), F32)]
        + [(half_shape, BF16)] * 2
        + [((z.p // 2, rows + z.tok, z.pb), BF16)] * 2,
        scalars, *x_pieces, *dy_pieces, w_gate, w_up, hg,
        scratch=[pltpu.VMEM((rows, z.d), BF16), pltpu.VMEM((z.tok, z.d), BF16)],
        flops=4 * rows * z.d * z.f,
    )
    got = []
    for k in range(z.inner - 1, -1, -1):
        (part,) = call(
            functools.partial(first_back, z, k),
            [((z.n, z.r, z.cb), BF16 if k else F32)],
            scalars, acts, w_gate, w_up, flops=4 * z.tok * z.d * z.f // z.inner, limit=6815744,
        )
        got.append(lax.ppermute(part, "tensor", xor_pairs(z.n, k)) if k else part)
    (half,) = run(
        sum_inner, [((z.n, z.r, z.cb), BF16)], scalars, got[-1], *got[-2::-1], flops=PREFETCH
    )
    crossed = []
    for o in range(z.outer):
        pairs = [
            (a * z.n + i, (a - 1) % z.p * z.n + (i ^ (o * z.inner)))
            for a in range(z.p)
            for i in range(z.n)
        ]
        crossed.append(lax.ppermute(half, ("pipe", "tensor"), pairs))
    (block,) = run(
        sum_outer, [((z.n, z.r, z.cb), BF16)], scalars, *crossed, flops=PREFETCH
    )
    blocks = [block] + [
        lax.ppermute(block, "tensor", xor_pairs(z.n, k)) for k in range(1, z.inner)
    ]
    loss_pieces = spread_rows(
        after(loss_grad[None], half), z, scalars, sections=[z.p - 1], gate=blocks[1]
    )
    acts_two, back, near_two, far_two, dy_even, dy_odd = run(
        second_hidden,
        [((2 * z.tok, z.f), BF16), ((z.r, z.d), BF16)]
        + [((z.tok, z.f), BF16)] * 2
        + [((z.p // 2, z.tok, z.pb), BF16)] * 2,
        scalars, *blocks, *loss_pieces, w_down, a_next, b_next,
        scratch=[pltpu.VMEM((z.tok, z.d), BF16)], flops=2 * z.tok * z.d * z.f,
    )
    returned = lax.ppermute(back, "pipe", [(a, (a + 1) % z.p) for a in range(z.p)])
    own, *sent = run(
        second_back,
        [((z.outer, z.r, z.d), BF16 if k else F32) for k in range(z.inner)],
        scalars, acts_two, w_gate, w_up, flops=4 * z.tok * z.d * z.f, limit=6815744,
    )
    got = [lax.ppermute(v, "tensor", xor_pairs(z.n, k + 1)) for k, v in enumerate(sent)]
    kept, *sent = run(
        sum_rows, [((z.r, z.d), F32)] + [((z.r, z.d), BF16)] * (z.outer - 1), scalars, own, *got
    )
    got = [
        lax.ppermute(v, "tensor", xor_pairs(z.n, (o + 1) * z.inner)) for o, v in enumerate(sent)
    ]
    (input_grads,) = run(
        finish_rows, [((z.ticks, 1, z.r, z.d), BF16)], scalars, returned, kept, *got
    )

    x_cols = share_columns(z, scalars, x_even, x_odd, gate=blocks[1])
    near, far = share_halves(z, scalars, near, far, gate=blocks[1])
    dy_cols = share_columns(z, scalars, dy_even, dy_odd)
    near_two, far_two = share_halves(z, scalars, near_two, far_two)
    (grad_down,) = call_grad(
        functools.partial(down_grad, z), (z.f, z.pb), 1, [(rows, z.f), (rows, z.pb)],
        scalars, near, far, x_cols, dy_cols,
    )
    grad_gate, grad_up = call_grad(
        functools.partial(in_grad, z), (z.pb, z.f), 2, [(2, rows, z.f)],
        scalars, near, far, near_two, far_two, x_cols,
    )
    return input_grads, grad_gate, grad_up, grad_down


def solution(mesh):
    placed = (
        P("pipe", None, "tensor", None),
        P("pipe", None, "tensor"),
        P("pipe", None, "tensor"),
        P("pipe", "tensor", None),
        P("pipe", "tensor", None),
        P("tensor", None),
        P(),
        P(),
    )
    return jax.shard_map(
        local,
        mesh=mesh,
        in_specs=placed,
        out_specs=(
            P(None, "pipe", "tensor", None),
            P("pipe", "tensor"),
            P("pipe", "tensor"),
            P("tensor", "pipe"),
        ),
        check_vma=False,
    )
```
